32 devices in a mesh: groups: 2 (over y), site: 4 (over z), sample: 4 (over x, core).
Axes of the slice: x: 2, y: 2, z: 4, core: 2. Of those that a mesh axis runs over, the one named last changes fastest.
Arguments:
- site_tensor: bfloat16 [8, 2048, 2, 2048], P(('groups', 'site'), None, None, 'sample'), parts along dimension 0, may hold values from -0.25 to 0.25
- fronts_in: bfloat16 [3072, 2048], P(('groups', 'sample')), parts along dimension 0
- outcomes: int32 [8, 1536], P(('groups', 'site'), 'sample'), parts along dimension 0, may hold values from 0 to 1
- charges: int32 [10, 16], P('groups'), parts along dimension 0, may hold values from 0 to 3
Outputs:
- fronts_out: bfloat16 [8, 1536, 2048], P(('groups', 'site'), 'sample'), parts along dimension 0
- log_steps: float32 [8, 1536], P(('groups', 'site'), 'sample'), parts along dimension 0
The draws below stay inside these ranges and needn't reach their ends.
There are 2 independent parts, one for each index of `groups`. The reference program is written for one: setup_inputs(seed, part) draws one part's arguments, and reference() takes and returns one part's arrays. A program takes and returns all parts, laid end to end along the dimension named above; each array names one. Nothing has to cross between parts.
All inputs are finite; a program needn't handle non-finite values.
Results may differ from the reference program's by a relative error of at most 0.012.
Values may be sent and summed in bfloat16 or wider, within the bound.
No kernel may reach another device: no remote copies, remote signals or barrier semaphores. Data moves between devices by JAX's collectives and lax.ppermute only.
A program may use at most 128 MiB of HBM per device.

```python
import jax
import jax.numpy as jnp
from jax import lax

BOND = 2048
BLOCK = 128
CHARGES = 4
PHYS = 2
NB = 16
SITES = 4
ROWS = 1536


def draw_fronts_in(key, part):
    values = jax.random.normal(jax.random.fold_in(key, 11), (ROWS, BOND), jnp.float32)
    return jnp.clip(values, -8.0, 8.0).astype(jnp.bfloat16)


def plant(result, key, least, largest):
    longest = result.shape.index(max(result.shape))
    spots = []
    for shift in (0, 1):
        where = [jax.random.randint(jax.random.fold_in(key, axis), (), 0, length) for axis, length in enumerate(result.shape)]
        where[longest] = (where[longest] + shift) % result.shape[longest]
        spots.append(tuple(where))
    return result.at[spots[0]].set(least).at[spots[1]].set(largest)


def block_scale(rng, shape, cuts, smallest, largest):
    level, own = 1.0, jax.random.fold_in(rng, 6)
    for position, blocks in cuts:
        heights = jnp.exp(jax.random.uniform(jax.random.fold_in(own, position), (blocks,), jnp.float32, smallest / len(cuts), largest / len(cuts)))
        level = level * jnp.repeat(heights, shape[position] // blocks).reshape([-1 if axis == position else 1 for axis in range(len(shape))])
    return level


def noise(own_key, shape, width, bound, pieces=(), kind=jnp.bfloat16):
    entries = jax.random.normal(own_key, shape, jnp.float32) * width
    if len(pieces) > 0:
        entries = block_scale(own_key, shape, pieces, -0.22, 0.18) * entries
    return jnp.clip(entries, min=-bound, max=bound).astype(kind)


def setup_inputs(seed: int = 0, part: int = 0) -> dict:
    streams_of = jax.random.split(jax.random.key(seed), 5)
    part_splits = jax.random.split(jax.random.fold_in(streams_of[4], part), 5)
    site_tensor = noise(part_splits[0], (SITES, BOND, PHYS, BOND), (BOND // 4) ** -0.5, 0.25, ((0, 4), (3, 4)))
    fronts_in = draw_fronts_in(jax.random.fold_in(jax.random.fold_in(streams_of[4], part), 71), part)
    outcomes = plant(jax.random.randint(part_splits[2], (SITES, ROWS), 0, 2), jax.random.fold_in(part_splits[2], 1), 0, 1).astype(jnp.int32)
    charges = plant(jax.random.randint(part_splits[3], (SITES + 1, NB), 0, CHARGES), jax.random.fold_in(part_splits[3], 1), 0, CHARGES - 1).astype(jnp.int32)
    return dict(site_tensor=site_tensor, fronts_in=fronts_in, outcomes=outcomes, charges=charges)


epsilon = 1e-06

def block_mask(left_charge, right_charge):
    phases = jnp.arange(2, dtype=jnp.int32)
    return right_charge[None, None, :] == (left_charge[:, None, None] + phases[None, :, None]) % CHARGES

def reference(site_tensor, fronts_in, outcomes, charges):

    def one_site(front_rows, site_idx):
        tensor = lax.dynamic_index_in_dim(site_tensor, site_idx, 0, keepdims=False)
        left_charge = lax.dynamic_index_in_dim(charges, site_idx, 0, keepdims=False)
        right_charge = lax.dynamic_index_in_dim(charges, site_idx + 1, 0, keepdims=False)
        allowed = block_mask(left_charge, right_charge).astype(tensor.dtype)
        masked = (tensor.reshape(NB, BLOCK, 2, NB, BLOCK) * allowed[:, None, :, :, None]).reshape(BOND, 2 * BOND)
        products = jnp.dot(front_rows, masked, preferred_element_type=jnp.float32).reshape(ROWS, 2, BOND)
        picks = lax.dynamic_index_in_dim(outcomes, site_idx, 0, keepdims=False)
        chosen = jnp.where(picks[:, None] == 1, products[:, 1], products[:, 0])
        row_norm = jnp.sqrt(lax.optimization_barrier(jnp.mean(chosen * chosen, axis=1)) + epsilon)
        new_front = (chosen / row_norm[:, None]).astype(jnp.bfloat16)
        return (new_front, (new_front, jnp.log(row_norm)))
    final_front, outputs = lax.scan(one_site, fronts_in, jnp.arange(SITES, dtype=jnp.int32))
    return (outputs[0], outputs[1])
```

```python
import functools

import jax
import jax.numpy as jnp
from jax import lax
from jax.experimental import pallas as pl
from jax.experimental.pallas import tpu as pltpu
from jax.sharding import PartitionSpec as P

BLOCK = 128
CHARGES = 4
LANES = 128
EPSILON = 1e-06
CHUNKS = 4
MICRO = 48
DELAY = 2


def pick_kernel(code_ref, tensor_ref, out_ref):
    step = pl.program_id(0)
    rows = out_ref.shape[0]
    row = lax.broadcasted_iota(jnp.int32, (BLOCK, 2 * BLOCK), 0)
    col = lax.broadcasted_iota(jnp.int32, (BLOCK, 2 * BLOCK), 1)
    for b in range(rows // BLOCK):
        for j in range(out_ref.shape[1] // BLOCK):
            outcome = code_ref[step * (rows // BLOCK) + b, j]
            here = slice(b * BLOCK, (b + 1) * BLOCK)
            there = slice(j * BLOCK, (j + 1) * BLOCK)
            pairs = tensor_ref[0, here, :, there].reshape(2 * BLOCK, BLOCK)
            select = jnp.where((col == 2 * row + outcome) & (outcome < 2), 1.0, 0.0)
            out_ref[here, there] = jnp.dot(
                select.astype(jnp.bfloat16), pairs, preferred_element_type=jnp.float32
            ).astype(jnp.bfloat16)


def pick(tensor, code, chunk, chunks):
    _, bond, phys, width = tensor.shape
    depth = bond // chunks
    rows = 2 * BLOCK
    first = chunk * (depth // rows)
    return pl.pallas_call(
        pick_kernel,
        out_shape=jax.ShapeDtypeStruct((depth, width), tensor.dtype),
        grid_spec=pltpu.PrefetchScalarGridSpec(
            num_scalar_prefetch=1,
            grid=(depth // rows,),
            in_specs=[pl.BlockSpec((1, rows, phys, width), lambda i, c: (0, first + i, 0, 0))],
            out_specs=pl.BlockSpec((rows, width), lambda i, c: (i, 0)),
        ),
        cost_estimate=pl.CostEstimate(
            flops=4 * depth * width * BLOCK, bytes_accessed=6 * depth * width, transcendentals=0
        ),
    )(lax.slice_in_dim(code, chunk * (depth // BLOCK), (chunk + 1) * (depth // BLOCK)), tensor)


def join_kernel(shards, shard_ref, *refs):
    out_ref = refs[shards]
    for d in range(shards):
        width = refs[d].shape[1]
        there = pl.ds(pl.multiple_of(shard_ref[d] * width, BLOCK), width)
        out_ref[:, there] = refs[d][...]


def join(parts, shard_of):
    shards = len(parts)
    depth, width = parts[0].shape
    vmem = pl.BlockSpec(memory_space=pltpu.VMEM)
    return pl.pallas_call(
        functools.partial(join_kernel, shards),
        out_shape=pltpu.VMEM((depth, shards * width), parts[0].dtype),
        grid_spec=pltpu.PrefetchScalarGridSpec(
            num_scalar_prefetch=1, grid=(1,), in_specs=[vmem] * shards, out_specs=vmem
        ),
        cost_estimate=pl.CostEstimate(
            flops=0, bytes_accessed=4 * depth * width * shards, transcendentals=0
        ),
    )(shard_of, *parts)


def step_kernel(
    chunks, at, place_ref, right_ref, first_ref, received_ref, picks_ref, left_ref, *rest,
):
    weights = rest[:chunks]
    _, _, sent_ref, fronts_ref, norms_ref = rest[chunks : chunks + 5]
    lhs_ref, acc_ref, norm_ref, sems = rest[chunks + 5 :]
    rows, bond = sent_ref.shape
    depth = weights[0].shape[0]
    tile = min(bond, 512)

    @pl.when(place_ref[at + 1] == 1)
    def _():
        start = place_ref[at + 2]
        front = jnp.where(
            place_ref[at + 3] == 0,
            first_ref[...].astype(jnp.float32),
            received_ref[...].astype(jnp.float32),
        )
        charge = (left_ref[...] + picks_ref[...]) & (CHARGES - 1)
        for q in range(CHARGES):
            lhs_ref[q * rows : (q + 1) * rows, :] = jnp.where(charge == q, front, 0.0).astype(
                jnp.bfloat16
            )
        for n in range(bond // tile):
            here = slice(n * tile, (n + 1) * tile)
            total = jnp.zeros((CHARGES * rows, tile), jnp.float32)
            for c in range(chunks):
                total += jnp.dot(
                    lhs_ref[:, c * depth : (c + 1) * depth],
                    weights[c][:, here],
                    preferred_element_type=jnp.float32,
                )
            acc_ref[:, here] = total

        def chosen(j):
            first = pl.multiple_of(right_ref[j] * rows, 8)
            return acc_ref[pl.ds(first, rows), j * BLOCK : (j + 1) * BLOCK]

        squares = jnp.zeros((rows, LANES), jnp.float32)
        for j in range(bond // BLOCK):
            squares += chosen(j) * chosen(j)
        norm = jnp.sqrt(jnp.sum(squares, axis=1, keepdims=True) / bond + EPSILON)
        norm_ref[...] = jnp.broadcast_to(norm, norm_ref.shape)
        for j in range(bond // BLOCK):
            sent_ref[:, j * BLOCK : (j + 1) * BLOCK] = (chosen(j) / norm).astype(sent_ref.dtype)
        where = pl.ds(pl.multiple_of(start, 8), rows)
        copies = (
            pltpu.make_async_copy(sent_ref, fronts_ref.at[where], sems.at[0]),
            pltpu.make_async_copy(norm_ref, norms_ref.at[where], sems.at[1]),
        )
        for copy in copies:
            copy.start()
        for copy in copies:
            copy.wait()


def advance(at, place, right, first, received, picks, left, weights, fronts, norms):
    bond = fronts.shape[1]
    rows = received.shape[0]
    count = len(weights)
    vmem = pl.BlockSpec(memory_space=pltpu.VMEM)
    hbm = pl.BlockSpec(memory_space=pl.ANY)
    return pl.pallas_call(
        functools.partial(step_kernel, count, at),
        out_shape=(
            jax.ShapeDtypeStruct((rows, bond), jnp.bfloat16),
            jax.ShapeDtypeStruct(fronts.shape, fronts.dtype),
            jax.ShapeDtypeStruct(norms.shape, norms.dtype),
        ),
        grid_spec=pltpu.PrefetchScalarGridSpec(
            num_scalar_prefetch=2,
            grid=(1,),
            in_specs=[
                pl.BlockSpec((rows, bond), lambda i, place, *_: (place[at], 0)),
                vmem,
                pl.BlockSpec((rows, 1), lambda i, place, *_: (place[at], 0)),
                vmem,
                *[vmem] * count,
                hbm,
                hbm,
            ],
            out_specs=(vmem, hbm, hbm),
            scratch_shapes=[
                pltpu.VMEM((CHARGES * rows, bond), jnp.bfloat16),
                pltpu.VMEM((CHARGES * rows, bond), jnp.float32),
                pltpu.VMEM((rows, LANES), jnp.float32),
                pltpu.SemaphoreType.DMA((2,)),
            ],
        ),
        input_output_aliases={6 + count: 1, 7 + count: 2},
        compiler_params=pltpu.CompilerParams(vmem_limit_bytes=24 * 1024 * 1024),
        cost_estimate=pl.CostEstimate(
            flops=2 * CHARGES * rows * bond * bond,
            bytes_accessed=2 * bond * bond,
            transcendentals=0,
        ),
    )(place, right, first, received, picks, left, *weights, fronts, norms)


def gather_weights(site_tensor, code):
    count = lax.axis_size("sample")
    me = lax.axis_index("sample")
    cores = 2 if count % 2 == 0 else 1
    chips = count // cores
    chip, core = me // cores, me % cores
    own = [pick(site_tensor, code, chunk, CHUNKS) for chunk in range(CHUNKS)]
    by_shard, shard_of = [], []
    for far in range(chips):
        pairs = [(i, ((i // cores - far) % chips) * cores + i % cores) for i in range(count)]
        held = own if far == 0 else [lax.ppermute(part, "sample", pairs) for part in own]
        from_chip = (chip + far) % chips
        by_shard.append(held)
        shard_of.append(from_chip * cores + core)
        if cores == 2:
            swap = [(i, i ^ 1) for i in range(count)]
            by_shard.append([lax.ppermute(part, "sample", swap) for part in held])
            shard_of.append(from_chip * cores + (1 - core))
    return by_shard, jnp.stack(shard_of).astype(jnp.int32)


def per_device(site_tensor, fronts_in, outcomes, charges):
    owner = lax.axis_index("site")
    sites = lax.axis_size("site")
    me = lax.axis_index("sample")
    left = lax.dynamic_index_in_dim(charges, owner, 0, keepdims=False)
    right = lax.dynamic_index_in_dim(charges, owner + 1, 0, keepdims=False)
    row_count, bond = fronts_in.shape
    width = site_tensor.shape[3]
    per_shard = width // BLOCK
    own_right = lax.dynamic_slice_in_dim(right, me * per_shard, per_shard)
    code = (own_right[None, :] - left[:, None]) & (CHARGES - 1)
    by_shard, shard_of = gather_weights(site_tensor, code)
    weights = [join([shard[c] for shard in by_shard], shard_of) for c in range(CHUNKS)]

    micro_rows = MICRO
    micro_count = row_count // micro_rows
    picks = outcomes[0][:, None]
    left_lanes = jnp.repeat(left, BLOCK)[None, :]
    fronts = jnp.zeros((row_count, bond), jnp.bfloat16)
    norms = jnp.zeros((row_count, LANES), jnp.float32)
    received = {}
    steps = micro_count + DELAY * (sites - 1)
    micro = jnp.arange(steps, dtype=jnp.int32) - DELAY * owner
    active = (micro >= 0) & (micro < micro_count)
    micro = jnp.clip(micro, 0, micro_count - 1)
    place = jnp.stack(
        [micro, active.astype(jnp.int32), micro * micro_rows, jnp.full_like(micro, owner)], axis=1
    ).astype(jnp.int32).reshape(-1)
    for step in range(steps):
        incoming = received.pop(step - DELAY, None)
        if incoming is None:
            incoming = fronts_in[:micro_rows]
        sent, fronts, norms = advance(
            4 * step, place, right, fronts_in, incoming, picks, left_lanes,
            weights, fronts, norms,
        )
        pairs = [
            (s, s + 1) for s in range(sites - 1) if 0 <= step - DELAY * s < micro_count
        ]
        if pairs:
            received[step] = lax.ppermute(sent, "site", pairs)
    return fronts[None], jnp.log(norms[:, 0])[None]


def solution(mesh):
    in_specs = (
        P(("groups", "site"), None, None, "sample"),
        P(("groups", "sample"), None),
        P(("groups", "site"), "sample"),
        P("groups", None),
    )
    out_specs = (P(("groups", "site"), "sample", None), P(("groups", "site"), "sample"))
    return jax.shard_map(
        per_device, mesh=mesh, in_specs=in_specs, out_specs=out_specs, check_vma=False
    )
```

```python
import functools

import jax
import jax.numpy as jnp
from jax import lax
from jax.experimental import pallas as pl
from jax.experimental.pallas import tpu as pltpu
from jax.sharding import PartitionSpec as P

BLOCK = 128
CHARGES = 4
LANES = 128
EPSILON = 1e-06
MICRO = 48
DELAY = 3


VMEM = pl.BlockSpec(memory_space=pltpu.VMEM)
HBM = pl.BlockSpec(memory_space=pl.ANY)


def allowed_outcome(charge_ref, site, i, j):
    return (charge_ref[site + 1, j] - charge_ref[site, i]) & (CHARGES - 1)


def pick_kernel(blocks, charge_ref, tensor_ref, *refs):
    *out_refs, both_ref, packed_ref = refs
    width = both_ref.shape[2]
    per_shard = width // BLOCK
    site = lax.axis_index("site")
    mine = lax.axis_index("sample") * per_shard
    row = lax.broadcasted_iota(jnp.int32, (2 * BLOCK, 2 * BLOCK), 0)
    col = lax.broadcasted_iota(jnp.int32, (2 * BLOCK, 2 * BLOCK), 1)
    source = jnp.where(row < BLOCK, 2 * row, 2 * (row - BLOCK) + 1)
    select = jnp.where(col == source, 1.0, 0.0).astype(jnp.bfloat16)
    entry = jnp.int32(0)
    for i in range(blocks):
        slot = i % 2
        pairs = tensor_ref[0, i * BLOCK : (i + 1) * BLOCK, :, :]
        both_ref[slot] = jnp.dot(
            select, pairs.reshape(2 * BLOCK, width), preferred_element_type=jnp.float32
        ).astype(jnp.bfloat16)
        for j in range(per_shard):
            outcome = allowed_outcome(charge_ref, site, i, mine + j)
            start = pl.multiple_of(jnp.minimum(outcome, 1) * BLOCK, BLOCK)
            there = pl.ds(pl.multiple_of(entry * BLOCK, BLOCK), BLOCK)
            packed_ref[there, :] = both_ref[
                slot, pl.ds(start, BLOCK), j * BLOCK : (j + 1) * BLOCK
            ]
            entry += (outcome < 2).astype(jnp.int32)
    low = 0
    for out_ref in out_refs:
        high = low + out_ref.shape[0]
        out_ref[...] = packed_ref[low:high, :]
        low = high


def pick(tensor, charges, counts):
    _, bond, _, width = tensor.shape
    blocks = bond // BLOCK
    total = blocks * (width // BLOCK)
    return pl.pallas_call(
        functools.partial(pick_kernel, blocks),
        out_shape=tuple(
            jax.ShapeDtypeStruct((count * BLOCK, BLOCK), tensor.dtype) for count in counts
        ),
        grid_spec=pltpu.PrefetchScalarGridSpec(
            num_scalar_prefetch=1,
            grid=(1,),
            in_specs=[VMEM],
            out_specs=tuple(VMEM for _ in counts),
            scratch_shapes=[
                pltpu.VMEM((2, 2 * BLOCK, width), jnp.bfloat16),
                pltpu.VMEM(((total + 1) * BLOCK, BLOCK), jnp.bfloat16),
            ],
        ),
        compiler_params=pltpu.CompilerParams(vmem_limit_bytes=16 * 1024 * 1024),
        cost_estimate=pl.CostEstimate(
            flops=8 * bond * width * BLOCK, bytes_accessed=6 * bond * width, transcendentals=0
        ),
    )(charges, tensor)


def plan_kernel(blocks, per_shard, cores, charge_ref, table_ref):
    shards, _ = table_ref.shape
    chips = shards // cores
    me = lax.axis_index("sample")
    site = lax.axis_index("site")
    total = blocks * per_shard
    for d in range(shards):
        chip = lax.rem(me // cores + d // cores, chips)
        first = (chip * cores + lax.rem(me + d, cores)) * per_shard

        def one(i, entry):
            for j in range(per_shard):
                table_ref[d, entry] = i * (shards * per_shard) + first + j
                allowed = allowed_outcome(charge_ref, site, i, first + j) < 2
                entry += allowed.astype(jnp.int32)
            return entry

        count = lax.fori_loop(0, blocks, one, jnp.int32(0))
        table_ref[d, total + 1] = count


def plan(charges, blocks, per_shard, cores, shards):
    size = blocks * per_shard + 2
    return pl.pallas_call(
        functools.partial(plan_kernel, blocks, per_shard, cores),
        out_shape=jax.ShapeDtypeStruct((shards, size), jnp.int32),
        grid_spec=pltpu.PrefetchScalarGridSpec(
            num_scalar_prefetch=1,
            grid=(1,),
            in_specs=[],
            out_specs=pl.BlockSpec(memory_space=pltpu.SMEM),
        ),
        compiler_params=pltpu.CompilerParams(vmem_limit_bytes=1024 * 1024),
        cost_estimate=pl.CostEstimate(flops=100, bytes_accessed=4096, transcendentals=0),
    )(charges)


def place_blocks(table_ref, refs, out_ref, first):
    across = out_ref.shape[1] // BLOCK
    total = table_ref.shape[1] - 2
    for d, ref in enumerate(refs):
        count = table_ref[d, total + 1]

        def one(e, carry):
            spot = table_ref[d, first + e]
            rows = pl.ds(pl.multiple_of((spot // across) * BLOCK, BLOCK), BLOCK)
            cols = pl.ds(pl.multiple_of(lax.rem(spot, across) * BLOCK, BLOCK), BLOCK)
            out_ref[rows, cols] = ref[pl.ds(pl.multiple_of(e * BLOCK, BLOCK), BLOCK), :]
            return carry

        size = ref.shape[0] // BLOCK
        lax.fori_loop(0, jnp.clip(count - first, 0, size), one, 0)


def unpack_kernel(shards, rest, extras, first, fresh, table_ref, *refs):
    refs = list(refs)
    pieces, refs = refs[:shards], refs[shards:]
    more, refs = refs[:rest], refs[rest:]
    refs = refs[extras:]
    if not fresh:
        refs = refs[1:]
    out_ref, scratch = refs[0], refs[1:]
    if fresh:
        out_ref[...] = jnp.zeros(out_ref.shape, out_ref.dtype)
    place_blocks(table_ref, pieces, out_ref, first)
    if rest:
        spare_ref, sem = scratch
        last = first + pieces[0].shape[0] // BLOCK
        total = table_ref.shape[1] - 2
        need = table_ref[0, total + 1] > last
        for d in range(1, shards):
            need |= table_ref[d, total + 1] > last

        @pl.when(need)
        def _():
            for d in range(shards):
                copy = pltpu.make_async_copy(more[d], spare_ref.at[d], sem)
                copy.start()
                copy.wait()
            place_blocks(table_ref, [spare_ref.at[d] for d in range(shards)], out_ref, last)


def unpack(table, pieces, more, extras, first, weights, bond):
    shards = len(pieces)
    fresh = weights is None
    operands = [*pieces, *more, *extras]
    in_specs = [VMEM] * shards + [HBM] * (len(more) + len(extras))
    aliases = {}
    if not fresh:
        operands.append(weights)
        in_specs.append(VMEM)
        aliases = {len(operands): 0}
    scratch = []
    if more:
        scratch = [pltpu.VMEM((shards, *more[0].shape), more[0].dtype), pltpu.SemaphoreType.DMA]
    return pl.pallas_call(
        functools.partial(unpack_kernel, shards, len(more), len(extras), first, fresh),
        out_shape=pltpu.VMEM((bond, bond), pieces[0].dtype),
        grid_spec=pltpu.PrefetchScalarGridSpec(
            num_scalar_prefetch=1,
            grid=(1,),
            in_specs=in_specs,
            out_specs=VMEM,
            scratch_shapes=scratch,
        ),
        input_output_aliases=aliases,
        compiler_params=pltpu.CompilerParams(vmem_limit_bytes=24 * 1024 * 1024),
        cost_estimate=pl.CostEstimate(
            flops=0, bytes_accessed=4 * shards * pieces[0].size, transcendentals=0
        ),
    )(table, *operands)


def step_kernel(chunks, at, relay, carried, place_ref, right_ref, *refs):
    refs = list(refs)
    first_ref, picks_ref, left_ref = refs[:3]
    weights = refs[3 : 3 + chunks]
    refs = refs[3 + chunks :]
    received_ref = refs.pop(0) if relay else None
    if carried:
        old_ref, old_norm_ref = refs[:2]
        refs = refs[4:]
    sent_ref, norm_ref, fronts_ref, norms_ref, lhs_ref, acc_ref, sems = refs
    rows, bond = sent_ref.shape
    tile = min(bond, 512)

    def copies():
        where = pl.ds(pl.multiple_of(place_ref[at - 4 + 2], 8), rows)
        return (
            pltpu.make_async_copy(old_ref, fronts_ref.at[where], sems.at[0]),
            pltpu.make_async_copy(old_norm_ref, norms_ref.at[where], sems.at[1]),
        )

    if carried:

        @pl.when(place_ref[at - 4 + 1] == 1)
        def _():
            for copy in copies():
                copy.start()

    @pl.when(place_ref[at + 1] == 1)
    def _():
        here = pl.ds(pl.multiple_of(place_ref[at + 2], 8), rows)
        front = first_ref[here, :].astype(jnp.float32)
        if relay:
            front = jnp.where(
                place_ref[at + 3] == 0, front, received_ref[...].astype(jnp.float32)
            )
        charge = (left_ref[...] + picks_ref[here, :]) & (CHARGES - 1)
        for q in range(CHARGES):
            lhs_ref[q * rows : (q + 1) * rows, :] = jnp.where(charge == q, front, 0.0).astype(
                jnp.bfloat16
            )
        for n in range(bond // tile):
            cols = slice(n * tile, (n + 1) * tile)
            total = jnp.zeros((CHARGES * rows, tile), jnp.float32)
            low = 0
            for part in weights:
                high = low + part.shape[0]
                total += jnp.dot(
                    lhs_ref[:, low:high], part[:, cols], preferred_element_type=jnp.float32
                )
                low = high
            acc_ref[:, cols] = total

        def chosen(j):
            first = pl.multiple_of(right_ref[j] * rows, 8)
            return acc_ref[pl.ds(first, rows), j * BLOCK : (j + 1) * BLOCK]

        squares = jnp.zeros((rows, LANES), jnp.float32)
        for j in range(bond // BLOCK):
            squares += chosen(j) * chosen(j)
        norm = jnp.sqrt(jnp.sum(squares, axis=1, keepdims=True) / bond + EPSILON)
        norm_ref[...] = jnp.broadcast_to(norm, norm_ref.shape)
        for j in range(bond // BLOCK):
            sent_ref[:, j * BLOCK : (j + 1) * BLOCK] = (chosen(j) / norm).astype(sent_ref.dtype)

    if carried:

        @pl.when(place_ref[at - 4 + 1] == 1)
        def _():
            for copy in copies():
                copy.wait()


def advance(step, place, right, fronts_in, picks, left, weights, received, old, results):
    row_count, bond = fronts_in.shape
    rows = MICRO
    relay = received is not None
    carried = results is not None
    operands = [fronts_in, picks, left, *weights]
    in_specs = [VMEM] * len(operands)
    aliases = {}
    if relay:
        operands.append(received)
        in_specs.append(VMEM)
    if carried:
        operands += [*old, *results]
        in_specs += [VMEM, VMEM, HBM, HBM]
        aliases = {len(operands): 2, len(operands) + 1: 3}
    return pl.pallas_call(
        functools.partial(step_kernel, len(weights), 4 * step, relay, carried),
        out_shape=(
            jax.ShapeDtypeStruct((rows, bond), jnp.bfloat16),
            jax.ShapeDtypeStruct((rows, LANES), jnp.float32),
            jax.ShapeDtypeStruct((row_count, bond), jnp.bfloat16),
            jax.ShapeDtypeStruct((row_count, LANES), jnp.float32),
        ),
        grid_spec=pltpu.PrefetchScalarGridSpec(
            num_scalar_prefetch=2,
            grid=(1,),
            in_specs=in_specs,
            out_specs=(VMEM, VMEM, HBM, HBM),
            scratch_shapes=[
                pltpu.VMEM((CHARGES * rows, bond), jnp.bfloat16),
                pltpu.VMEM((CHARGES * rows, bond), jnp.float32),
                pltpu.SemaphoreType.DMA((2,)),
            ],
        ),
        input_output_aliases=aliases,
        compiler_params=pltpu.CompilerParams(vmem_limit_bytes=24 * 1024 * 1024),
        cost_estimate=pl.CostEstimate(
            flops=2 * CHARGES * rows * bond * bond,
            bytes_accessed=2 * bond * bond,
            transcendentals=0,
        ),
    )(place, right, *operands)


def finish_kernel(at, place_ref, old_ref, old_norm_ref, _, __, fronts_ref, norms_ref, sems):
    rows = old_ref.shape[0]

    @pl.when(place_ref[at + 1] == 1)
    def _():
        where = pl.ds(pl.multiple_of(place_ref[at + 2], 8), rows)
        copies = (
            pltpu.make_async_copy(old_ref, fronts_ref.at[where], sems.at[0]),
            pltpu.make_async_copy(old_norm_ref, norms_ref.at[where], sems.at[1]),
        )
        for copy in copies:
            copy.start()
        for copy in copies:
            copy.wait()


def finish(step, place, old, results):
    return pl.pallas_call(
        functools.partial(finish_kernel, 4 * step),
        out_shape=tuple(jax.ShapeDtypeStruct(r.shape, r.dtype) for r in results),
        grid_spec=pltpu.PrefetchScalarGridSpec(
            num_scalar_prefetch=1,
            grid=(1,),
            in_specs=[VMEM, VMEM, HBM, HBM],
            out_specs=(HBM, HBM),
            scratch_shapes=[pltpu.SemaphoreType.DMA((2,))],
        ),
        input_output_aliases={3: 0, 4: 1},
        compiler_params=pltpu.CompilerParams(vmem_limit_bytes=4 * 1024 * 1024),
    )(place, *old, *results)


def gather_weights(site_tensor, charges, extras):
    shards = lax.axis_size("sample")
    sites = lax.axis_size("site")
    groups = lax.axis_size("groups")
    cores = 2 if shards % 2 == 0 else 1
    chips = shards // cores
    bond = site_tensor.shape[1]
    blocks = bond // BLOCK
    per_shard = site_tensor.shape[3] // BLOCK
    total = blocks * per_shard
    size = total // 4
    counts = [size, size, size, total - 3 * size]
    cap = 3 * size
    swap = [(i, i ^ 1) for i in range(shards)]

    def across_chips(part):
        return [
            lax.ppermute(
                part,
                "sample",
                [(i, ((i // cores - hop) % chips) * cores + i % cores) for i in range(shards)],
            )
            for hop in range(1, chips)
        ]

    def across_cores(part):
        return [lax.ppermute(part, "sample", swap)] if cores == 2 else []

    own = pick(site_tensor, charges, counts)
    far = []
    for c in range(3):
        far.append(across_chips(own[c]))

    table = plan(charges, blocks, per_shard, cores, shards)
    outcome = (charges[1:, None, :] - charges[:-1, :, None]) & (CHARGES - 1)
    held = jnp.sum((outcome < 2).reshape(sites, blocks, shards, per_shard), axis=(1, 3))
    most = jnp.max(held.astype(jnp.int32)).reshape(1)
    for hop in range(1, groups):
        pairs = [(i, (i + hop) % groups) for i in range(groups)]
        most = jnp.maximum(most, lax.ppermute(jnp.max(held).astype(jnp.int32).reshape(1), "groups", pairs))

    def send_rest(part):
        parts = [part, *across_chips(part)]
        parts = [parts[:1] + across_cores(parts[0])] + [[p] + across_cores(p) for p in parts[1:]]
        return tuple(p for pair in parts for p in pair)[1:]

    def keep(part):
        return tuple(jnp.zeros_like(part) for _ in range(shards - 1))

    rest = [own[3], *lax.cond(most[0] > cap, send_rest, keep, own[3])]
    weights = None
    for c in range(3):
        parts = [own[c], *far[c]]
        if weights is not None:
            parts, weights = lax.optimization_barrier((parts, weights))
        pieces = []
        for part in parts:
            pieces += [part, *across_cores(part)]
        weights = unpack(
            table, pieces, rest if c == 2 else [], [*extras, *rest] if c == 0 else [],
            c * size, weights, bond,
        )
    return [weights]


def pipeline(site_tensor, fronts_in, outcomes, charges):
    owner = lax.axis_index("site")
    sites = lax.axis_size("site")
    left = lax.dynamic_index_in_dim(charges, owner, 0, keepdims=False)
    right = lax.dynamic_index_in_dim(charges, owner + 1, 0, keepdims=False)
    row_count, _ = fronts_in.shape
    micro_count = row_count // MICRO
    picks = outcomes[0][:, None]
    left_lanes = jnp.repeat(left, BLOCK)[None, :]
    steps = micro_count + DELAY * (sites - 1)
    micro = jnp.arange(steps, dtype=jnp.int32) - DELAY * owner
    active = (micro >= 0) & (micro < micro_count)
    micro = jnp.clip(micro, 0, micro_count - 1)
    place = jnp.stack(
        [micro, active.astype(jnp.int32), micro * MICRO, jnp.full_like(micro, owner)], axis=1
    ).astype(jnp.int32).reshape(-1)

    weights = gather_weights(site_tensor, charges, [place, picks, left_lanes, right])
    received, old, results = {}, None, None
    for step in range(steps):
        sent, norm, *results = advance(
            step, place, right, fronts_in, picks, left_lanes, weights,
            received.pop(step - DELAY, None), old, results,
        )
        old = (sent, norm)
        pairs = [
            (s, s + 1) for s in range(sites - 1) if 0 <= step - DELAY * s < micro_count
        ]
        if pairs:
            received[step] = lax.ppermute(sent, "site", pairs)
    fronts, norms = finish(steps - 1, place, old, results)
    return fronts[None], jnp.log(norms[:, 0])[None]


def solution(mesh):
    in_specs = (
        P(("groups", "site"), None, None, "sample"),
        P(("groups", "sample"), None),
        P(("groups", "site"), "sample"),
        P("groups", None),
    )
    out_specs = (P(("groups", "site"), "sample", None), P(("groups", "site"), "sample"))
    return jax.shard_map(
        pipeline, mesh=mesh, in_specs=in_specs, out_specs=out_specs, check_vma=False
    )
```

```python
import functools

import jax
import jax.numpy as jnp
from jax import lax
from jax.experimental import pallas as pl
from jax.experimental.pallas import tpu as pltpu
from jax.sharding import PartitionSpec as P

BLOCK = 128
CHARGES = 4
LANES = 128
EPSILON = 1e-06
MICRO = 48
DELAY = 3


VMEM = pl.BlockSpec(memory_space=pltpu.VMEM)
HBM = pl.BlockSpec(memory_space=pl.ANY)


def allowed_outcome(charge_ref, site, i, j):
    return (charge_ref[site + 1, j] - charge_ref[site, i]) & (CHARGES - 1)


def pick_kernel(blocks, starts, charge_ref, tensor_ref, packed_ref, *refs):
    *out_refs, both_ref = refs
    width = tensor_ref.shape[3]
    per_shard = width // BLOCK
    site = lax.axis_index("site")
    mine = lax.axis_index("sample") * per_shard
    row = lax.broadcasted_iota(jnp.int32, (2 * BLOCK, 2 * BLOCK), 0)
    col = lax.broadcasted_iota(jnp.int32, (2 * BLOCK, 2 * BLOCK), 1)
    source = jnp.where(row < BLOCK, 2 * row, 2 * (row - BLOCK) + 1)
    select = jnp.where(col == source, 1.0, 0.0).astype(jnp.bfloat16)
    both_ref[...] = select
    entry = jnp.int32(0)
    for i in range(blocks):
        pairs = tensor_ref[0, i * BLOCK : (i + 1) * BLOCK, :, :].reshape(2 * BLOCK, width)
        for j in range(per_shard):
            outcome = allowed_outcome(charge_ref, site, i, mine + j)
            start = pl.multiple_of(jnp.minimum(outcome, 1) * BLOCK, BLOCK)
            there = pl.ds(pl.multiple_of(entry * BLOCK, BLOCK), BLOCK)
            packed_ref[there, :] = jnp.dot(
                both_ref[pl.ds(start, BLOCK), :],
                pairs[:, j * BLOCK : (j + 1) * BLOCK],
                preferred_element_type=jnp.float32,
            ).astype(jnp.bfloat16)
            entry += (outcome < 2).astype(jnp.int32)
    for start, out_ref in zip(starts, out_refs):
        low = start * BLOCK
        out_ref[...] = packed_ref[low : low + out_ref.shape[0], :]


def pick(tensor, charges, spans):
    _, bond, _, width = tensor.shape
    blocks = bond // BLOCK
    total = blocks * (width // BLOCK)
    return pl.pallas_call(
        functools.partial(pick_kernel, blocks, [low for low, _ in spans]),
        out_shape=tuple(
            pltpu.VMEM((count * BLOCK, BLOCK), tensor.dtype)
            for count in (total + 1, *[high - low for low, high in spans])
        ),
        grid_spec=pltpu.PrefetchScalarGridSpec(
            num_scalar_prefetch=1,
            grid=(1,),
            in_specs=[VMEM],
            out_specs=(VMEM,) * (1 + len(spans)),
            scratch_shapes=[pltpu.VMEM((2 * BLOCK, 2 * BLOCK), jnp.bfloat16)],
        ),
        compiler_params=pltpu.CompilerParams(vmem_limit_bytes=16 * 1024 * 1024),
        cost_estimate=pl.CostEstimate(
            flops=8 * bond * width * BLOCK, bytes_accessed=6 * bond * width, transcendentals=0
        ),
    )(charges, tensor)


def plan_kernel(blocks, per_shard, cores, charge_ref, table_ref):
    shards, _ = table_ref.shape
    chips = shards // cores
    me = lax.axis_index("sample")
    site = lax.axis_index("site")
    total = blocks * per_shard
    for d in range(shards):
        chip = lax.rem(me // cores + d // cores, chips)
        first = (chip * cores + lax.rem(me + d, cores)) * per_shard

        def one(i, entry):
            for j in range(per_shard):
                table_ref[d, entry] = i * (shards * per_shard) + first + j
                allowed = allowed_outcome(charge_ref, site, i, first + j) < 2
                entry += allowed.astype(jnp.int32)
            return entry

        count = lax.fori_loop(0, blocks, one, jnp.int32(0))
        table_ref[d, total + 1] = count


def plan(charges, blocks, per_shard, cores, shards):
    size = blocks * per_shard + 2
    return pl.pallas_call(
        functools.partial(plan_kernel, blocks, per_shard, cores),
        out_shape=jax.ShapeDtypeStruct((shards, size), jnp.int32),
        grid_spec=pltpu.PrefetchScalarGridSpec(
            num_scalar_prefetch=1,
            grid=(1,),
            in_specs=[],
            out_specs=pl.BlockSpec(memory_space=pltpu.SMEM),
        ),
        compiler_params=pltpu.CompilerParams(vmem_limit_bytes=1024 * 1024),
        cost_estimate=pl.CostEstimate(flops=100, bytes_accessed=4096, transcendentals=0),
    )(charges)


def place_blocks(table_ref, d, first, ref, out_ref):
    across = out_ref.shape[1] // BLOCK
    total = table_ref.shape[1] - 2
    size = min(ref.shape[0] // BLOCK, total - first)

    def one(e, carry):
        spot = table_ref[d, first + e]
        rows = pl.ds(pl.multiple_of((spot // across) * BLOCK, BLOCK), BLOCK)
        cols = pl.ds(pl.multiple_of(lax.rem(spot, across) * BLOCK, BLOCK), BLOCK)
        out_ref[rows, cols] = ref[pl.ds(pl.multiple_of(e * BLOCK, BLOCK), BLOCK), :]
        return carry

    lax.fori_loop(0, jnp.clip(table_ref[d, total + 1] - first, 0, size), one, 0)


def unpack_kernel(pieces, extras, fresh, table_ref, *refs):
    refs = list(refs)
    held, refs = refs[: len(pieces)], refs[len(pieces) + extras + (0 if fresh else 1) :]
    out_ref, scratch = refs[0], refs[1:]
    first_site = lax.axis_index("site") == 0
    if fresh:
        out_ref[...] = jnp.zeros(out_ref.shape, out_ref.dtype)
    for ref, (d, first, kind) in zip(held, pieces):
        place = functools.partial(place_blocks, table_ref, d, first, out_ref=out_ref)
        if kind == "always":
            place(ref)
        elif kind == "rest":

            @pl.when(table_ref[d, table_ref.shape[1] - 1] > first)
            def _(ref=ref, place=place):
                spare_ref, sem = scratch
                copy = pltpu.make_async_copy(ref, spare_ref, sem)
                copy.start()
                copy.wait()
                place(spare_ref)

        else:

            @pl.when(first_site if kind == "first" else ~first_site)
            def _(ref=ref, place=place):
                place(ref)


def unpack(table, pieces, extras, weights, bond):
    fresh = weights is None
    operands = [piece[0] for piece in pieces] + list(extras)
    in_specs = [HBM if piece[3] == "rest" else VMEM for piece in pieces] + [HBM] * len(extras)
    aliases = {}
    if not fresh:
        operands.append(weights)
        in_specs.append(VMEM)
        aliases = {len(operands): 0}
    rest = [piece[0] for piece in pieces if piece[3] == "rest"]
    scratch = [pltpu.VMEM(rest[0].shape, rest[0].dtype), pltpu.SemaphoreType.DMA] if rest else []
    dtype = pieces[0][0].dtype
    return pl.pallas_call(
        functools.partial(unpack_kernel, [piece[1:] for piece in pieces], len(extras), fresh),
        out_shape=pltpu.VMEM((bond, bond), dtype),
        grid_spec=pltpu.PrefetchScalarGridSpec(
            num_scalar_prefetch=1,
            grid=(1,),
            in_specs=in_specs,
            out_specs=VMEM,
            scratch_shapes=scratch,
        ),
        input_output_aliases=aliases,
        compiler_params=pltpu.CompilerParams(vmem_limit_bytes=24 * 1024 * 1024),
        cost_estimate=pl.CostEstimate(
            flops=0,
            bytes_accessed=4 * sum(piece[0].size for piece in pieces if piece[3] != "rest"),
            transcendentals=0,
        ),
    )(table, *operands)


def blank(shape, dtype, count):
    return pl.pallas_call(
        lambda *refs: None,
        out_shape=(jax.ShapeDtypeStruct(shape, dtype),) * count,
        out_specs=(HBM,) * count,
        compiler_params=pltpu.CompilerParams(vmem_limit_bytes=1024 * 1024),
    )()


def step_kernel(chunks, at, relay, carried, ends, place_ref, right_ref, *refs):
    refs = list(refs)
    first_ref, picks_ref, left_ref = refs[:3]
    weights = refs[3 : 3 + chunks]
    refs = refs[3 + chunks :]
    received_ref = refs.pop(0) if relay else None
    if carried:
        old_ref, old_norm_ref = refs[:2]
        refs = refs[4:]
    sent_ref, norm_ref, fronts_ref, norms_ref, lhs_ref, acc_ref, sems = refs
    rows, bond = sent_ref.shape
    tile = min(bond, 512)

    def copies(back, front_ref, row_norm_ref):
        where = pl.ds(pl.multiple_of(place_ref[at - 4 * back + 2], 8), rows)
        return (
            pltpu.make_async_copy(front_ref, fronts_ref.at[where], sems.at[0]),
            pltpu.make_async_copy(row_norm_ref, norms_ref.at[where], sems.at[1]),
        )

    if carried:

        @pl.when(place_ref[at - 4 + 1] == 1)
        def _():
            for copy in copies(1, old_ref, old_norm_ref):
                copy.start()

    @pl.when(place_ref[at + 1] == 1)
    def _():
        here = pl.ds(pl.multiple_of(place_ref[at + 2], 8), rows)
        front = first_ref[here, :].astype(jnp.float32)
        if relay:
            front = jnp.where(
                place_ref[at + 3] == 0, front, received_ref[...].astype(jnp.float32)
            )
        charge = (left_ref[...] + picks_ref[here, :]) & (CHARGES - 1)
        for q in range(CHARGES):
            lhs_ref[q * rows : (q + 1) * rows, :] = jnp.where(charge == q, front, 0.0).astype(
                jnp.bfloat16
            )
        for n in range(bond // tile):
            cols = slice(n * tile, (n + 1) * tile)
            total = jnp.zeros((CHARGES * rows, tile), jnp.float32)
            low = 0
            for part in weights:
                high = low + part.shape[0]
                total += jnp.dot(
                    lhs_ref[:, low:high], part[:, cols], preferred_element_type=jnp.float32
                )
                low = high
            acc_ref[:, cols] = total

        def chosen(j):
            first = pl.multiple_of(right_ref[j] * rows, 8)
            return acc_ref[pl.ds(first, rows), j * BLOCK : (j + 1) * BLOCK]

        squares = jnp.zeros((rows, LANES), jnp.float32)
        for j in range(bond // BLOCK):
            squares += chosen(j) * chosen(j)
        norm = jnp.sqrt(jnp.sum(squares, axis=1, keepdims=True) / bond + EPSILON)
        norm_ref[...] = jnp.broadcast_to(norm, norm_ref.shape)
        for j in range(bond // BLOCK):
            sent_ref[:, j * BLOCK : (j + 1) * BLOCK] = (chosen(j) / norm).astype(sent_ref.dtype)

    if carried:

        @pl.when(place_ref[at - 4 + 1] == 1)
        def _():
            for copy in copies(1, old_ref, old_norm_ref):
                copy.wait()

    if ends:

        @pl.when(place_ref[at + 1] == 1)
        def _():
            for copy in copies(0, sent_ref, norm_ref):
                copy.start()
            for copy in copies(0, sent_ref, norm_ref):
                copy.wait()


def advance(step, ends, place, right, fronts_in, picks, left, weights, received, old, results):
    row_count, bond = fronts_in.shape
    rows = MICRO
    relay = received is not None
    carried = results is not None
    operands = [fronts_in, picks, left, *weights]
    in_specs = [VMEM] * len(operands)
    aliases = {}
    if relay:
        operands.append(received)
        in_specs.append(VMEM)
    if carried:
        operands += [*old, *results]
        in_specs += [VMEM, VMEM, HBM, HBM]
        aliases = {len(operands): 2, len(operands) + 1: 3}
    return pl.pallas_call(
        functools.partial(step_kernel, len(weights), 4 * step, relay, carried, ends),
        out_shape=(
            jax.ShapeDtypeStruct((rows, bond), jnp.bfloat16),
            jax.ShapeDtypeStruct((rows, LANES), jnp.float32),
            jax.ShapeDtypeStruct((row_count, bond), jnp.bfloat16),
            jax.ShapeDtypeStruct((row_count, LANES), jnp.float32),
        ),
        grid_spec=pltpu.PrefetchScalarGridSpec(
            num_scalar_prefetch=2,
            grid=(1,),
            in_specs=in_specs,
            out_specs=(VMEM, VMEM, HBM, HBM),
            scratch_shapes=[
                pltpu.VMEM((CHARGES * rows, bond), jnp.bfloat16),
                pltpu.VMEM((CHARGES * rows, bond), jnp.float32),
                pltpu.SemaphoreType.DMA((2,)),
            ],
        ),
        input_output_aliases=aliases,
        compiler_params=pltpu.CompilerParams(vmem_limit_bytes=24 * 1024 * 1024),
        cost_estimate=pl.CostEstimate(
            flops=2 * CHARGES * rows * bond * bond,
            bytes_accessed=2 * bond * bond,
            transcendentals=0,
        ),
    )(place, right, *operands)


def gather_weights(site_tensor, charges, extras):
    shards = lax.axis_size("sample")
    sites = lax.axis_size("site")
    groups = lax.axis_size("groups")
    cores = 2 if shards % 2 == 0 else 1
    chips = shards // cores
    bond = site_tensor.shape[1]
    blocks = bond // BLOCK
    per_shard = site_tensor.shape[3] // BLOCK
    total = blocks * per_shard
    unit = total // 16
    early, turn, cap = 6 * unit, 8 * unit, 12 * unit
    if sites == 1:
        turn = early
    spans = [(0, early), (early, turn), (turn, cap), (early, cap)]

    def to(hop, i):
        return ((i // cores - hop) % chips) * cores + i % cores

    def move(part, pairs):
        flat = [(s * shards + i, t * shards + j) for (s, i), (t, j) in pairs]
        return lax.ppermute(part, ("site", "sample"), flat)

    everyone = [(s, i) for s in range(sites) for i in range(shards)]

    def across_chips(part, up, among):
        return [
            move(part, [((s, i), (s + up, to(hop, i))) for s, i in everyone if s in among])
            for hop in range(1, chips)
        ]

    def across_cores(part):
        return lax.ppermute(part, "sample", [(i, i ^ 1) for i in range(shards)])

    def with_cores(parts, first, kind):
        pieces = []
        for hop, part in enumerate(parts, 1):
            pieces.append((part, hop * cores, first, kind))
            if cores == 2:
                pieces.append((across_cores(part), hop * cores + 1, first, kind))
        return pieces

    packed, head, detour, tail, late = pick(site_tensor, charges, spans)
    one, others = range(1), range(1, sites)
    head = across_chips(head, 0, range(sites))
    tail = across_chips(tail, 0, one)
    away = across_chips(detour, 1, one)
    late = across_chips(late, 0, others)

    table = plan(charges, blocks, per_shard, cores, shards)
    outcome = (charges[1:, None, :] - charges[:-1, :, None]) & (CHARGES - 1)
    held = jnp.sum((outcome < 2).reshape(sites, blocks, shards, per_shard), axis=(1, 3))
    mine = jnp.max(held.astype(jnp.int32)).reshape(1)
    most = mine
    for hop in range(1, groups):
        pairs = [(i, (i + hop) % groups) for i in range(groups)]
        most = jnp.maximum(most, lax.ppermute(mine, "groups", pairs))

    rest_shape = ((total - cap) * BLOCK, BLOCK)

    def send_rest(blocks):
        parts = across_chips(blocks[cap * BLOCK : total * BLOCK], 0, range(sites))
        return tuple(piece[0] for piece in with_cores(parts, cap, "rest"))

    def keep(blocks):
        return tuple(blank(rest_shape, blocks.dtype, (chips - 1) * cores))

    rest = lax.cond(most[0] > cap, send_rest, keep, packed) if chips > 1 else ()
    rest = [(part, cores + k, cap, "rest") for k, part in enumerate(rest)]

    local = [(packed, 0, 0, "always")]
    if cores == 2:
        local.append((across_cores(packed), 1, 0, "always"))
    weights = unpack(table, local, [*extras, *[piece[0] for piece in rest]], None, bond)

    home = [move(part, [((1, i), (0, i)) for i in range(shards)]) for part in away]
    (head, home), weights = lax.optimization_barrier(((head, home), weights))
    pieces = with_cores(head, 0, "always")
    pieces += with_cores(home, early, "first")
    weights = unpack(table, pieces, [], weights, bond)
    tail, weights = lax.optimization_barrier((tail, weights))
    pieces = with_cores(tail, turn, "first")
    weights = unpack(table, pieces + rest, [], weights, bond)

    def exchange(after):
        parts, after = lax.optimization_barrier((late, after))
        return with_cores(parts, early, "others")

    def complete(weights, pieces, after):
        return unpack(table, pieces, [after], weights, bond)

    return weights, exchange, complete


def pipeline(site_tensor, fronts_in, outcomes, charges):
    owner = lax.axis_index("site")
    sites = lax.axis_size("site")
    left = lax.dynamic_index_in_dim(charges, owner, 0, keepdims=False)
    right = lax.dynamic_index_in_dim(charges, owner + 1, 0, keepdims=False)
    row_count, _ = fronts_in.shape
    micro_count = row_count // MICRO
    picks = outcomes[0][:, None]
    left_lanes = jnp.repeat(left, BLOCK)[None, :]
    steps = micro_count + DELAY * (sites - 1)
    micro = jnp.arange(steps, dtype=jnp.int32) - DELAY * owner
    active = (micro >= 0) & (micro < micro_count)
    micro = jnp.clip(micro, 0, micro_count - 1)
    place = jnp.stack(
        [micro, active.astype(jnp.int32), micro * MICRO, jnp.full_like(micro, owner)], axis=1
    ).astype(jnp.int32).reshape(-1)

    weights, exchange, complete = gather_weights(site_tensor, charges, [place, picks, left_lanes, right])
    received, old, results = {}, None, None
    for step in range(steps):
        if step == DELAY - 1:
            late = exchange(old[0])
        if step == DELAY:
            weights = complete(weights, late, old[0])
        sent, norm, *results = advance(
            step, step == steps - 1, place, right, fronts_in, picks, left_lanes, [weights],
            received.pop(step - DELAY, None), old, results,
        )
        old = (sent, norm)
        pairs = [
            (s, s + 1) for s in range(sites - 1) if 0 <= step - DELAY * s < micro_count
        ]
        if pairs:
            received[step] = lax.ppermute(sent, "site", pairs)
    fronts, norms = results
    return fronts[None], jnp.log(norms[:, 0])[None]


def solution(mesh):
    in_specs = (
        P(("groups", "site"), None, None, "sample"),
        P(("groups", "sample"), None),
        P(("groups", "site"), "sample"),
        P("groups", None),
    )
    out_specs = (P(("groups", "site"), "sample", None), P(("groups", "site"), "sample"))
    return jax.shard_map(
        pipeline, mesh=mesh, in_specs=in_specs, out_specs=out_specs, check_vma=False
    )
```

```python
import functools

import jax
import jax.numpy as jnp
from jax import lax
from jax.experimental import pallas as pl
from jax.experimental.pallas import tpu as pltpu
from jax.sharding import PartitionSpec as P

BLOCK = 128
CHARGES = 4
LANES = 128
SHIFT = 12
EPSILON = 1e-06
MICRO = 48
DELAY = 3


VMEM = pl.BlockSpec(memory_space=pltpu.VMEM)
HBM = pl.BlockSpec(memory_space=pl.ANY)


def allowed_outcome(charge_ref, site, i, j):
    return (charge_ref[site + 1, j] - charge_ref[site, i]) & (CHARGES - 1)


def pick_kernel(blocks, starts, charge_ref, tensor_ref, packed_ref, *refs):
    *out_refs, both_ref = refs
    width = tensor_ref.shape[3]
    per_shard = width // BLOCK
    site = lax.axis_index("site")
    mine = lax.axis_index("sample") * per_shard
    row = lax.broadcasted_iota(jnp.int32, (2 * BLOCK, 2 * BLOCK), 0)
    col = lax.broadcasted_iota(jnp.int32, (2 * BLOCK, 2 * BLOCK), 1)
    source = jnp.where(row < BLOCK, 2 * row, 2 * (row - BLOCK) + 1)
    select = jnp.where(col == source, 1.0, 0.0).astype(jnp.bfloat16)
    both_ref[...] = select
    entry = jnp.int32(0)
    for i in range(blocks):
        pairs = tensor_ref[0, i * BLOCK : (i + 1) * BLOCK, :, :].reshape(2 * BLOCK, width)
        for j in range(per_shard):
            outcome = allowed_outcome(charge_ref, site, i, mine + j)
            start = pl.multiple_of(jnp.minimum(outcome, 1) * BLOCK, BLOCK)
            there = pl.ds(pl.multiple_of(entry * BLOCK, BLOCK), BLOCK)
            packed_ref[there, :] = jnp.dot(
                both_ref[pl.ds(start, BLOCK), :],
                pairs[:, j * BLOCK : (j + 1) * BLOCK],
                preferred_element_type=jnp.float32,
            ).astype(jnp.bfloat16)
            entry += (outcome < 2).astype(jnp.int32)
    for start, out_ref in zip(starts, out_refs):
        low = start * BLOCK
        out_ref[...] = packed_ref[low : low + out_ref.shape[0], :]


def pick(tensor, charges, spans):
    _, bond, _, width = tensor.shape
    blocks = bond // BLOCK
    total = blocks * (width // BLOCK)
    return pl.pallas_call(
        functools.partial(pick_kernel, blocks, [low for low, _ in spans]),
        out_shape=tuple(
            pltpu.VMEM((count * BLOCK, BLOCK), tensor.dtype)
            for count in (total + 1, *[high - low for low, high in spans])
        ),
        grid_spec=pltpu.PrefetchScalarGridSpec(
            num_scalar_prefetch=1,
            grid=(1,),
            in_specs=[VMEM],
            out_specs=(VMEM,) * (1 + len(spans)),
            scratch_shapes=[pltpu.VMEM((2 * BLOCK, 2 * BLOCK), jnp.bfloat16)],
        ),
        compiler_params=pltpu.CompilerParams(vmem_limit_bytes=16 * 1024 * 1024),
        cost_estimate=pl.CostEstimate(
            flops=8 * bond * width * BLOCK, bytes_accessed=6 * bond * width, transcendentals=0
        ),
    )(charges, tensor)


def plan_kernel(blocks, per_shard, cores, charge_ref, table_ref):
    shards, _ = table_ref.shape
    chips = shards // cores
    me = lax.axis_index("sample")
    site = lax.axis_index("site")
    total = blocks * per_shard
    for d in range(shards):
        chip = lax.rem(me // cores + d // cores, chips)
        first = (chip * cores + lax.rem(me + d, cores)) * per_shard

        def one(i, entry):
            for j in range(per_shard):
                table_ref[d, entry] = (i << SHIFT) + first + j
                allowed = allowed_outcome(charge_ref, site, i, first + j) < 2
                entry += allowed.astype(jnp.int32)
            return entry

        count = lax.fori_loop(0, blocks, one, jnp.int32(0))
        table_ref[d, total + 1] = count


def plan(charges, blocks, per_shard, cores, shards):
    size = blocks * per_shard + 2
    return pl.pallas_call(
        functools.partial(plan_kernel, blocks, per_shard, cores),
        out_shape=jax.ShapeDtypeStruct((shards, size), jnp.int32),
        grid_spec=pltpu.PrefetchScalarGridSpec(
            num_scalar_prefetch=1,
            grid=(1,),
            in_specs=[],
            out_specs=pl.BlockSpec(memory_space=pltpu.SMEM),
        ),
        compiler_params=pltpu.CompilerParams(vmem_limit_bytes=1024 * 1024),
        cost_estimate=pl.CostEstimate(flops=100, bytes_accessed=4096, transcendentals=0),
    )(charges)


def place_blocks(table_ref, d, first, ref, out_ref):
    total = table_ref.shape[1] - 2
    size = min(ref.shape[0] // BLOCK, total - first)

    def one(e, carry):
        spot = table_ref[d, first + e]
        rows = pl.ds(pl.multiple_of((spot >> SHIFT) * BLOCK, BLOCK), BLOCK)
        cols = pl.ds(pl.multiple_of((spot & ((1 << SHIFT) - 1)) * BLOCK, BLOCK), BLOCK)
        out_ref[rows, cols] = ref[pl.ds(pl.multiple_of(e * BLOCK, BLOCK), BLOCK), :]
        return carry

    lax.fori_loop(0, jnp.clip(table_ref[d, total + 1] - first, 0, size), one, 0)


def unpack_kernel(pieces, extras, fresh, table_ref, *refs):
    refs = list(refs)
    held, refs = refs[: len(pieces)], refs[len(pieces) + extras + (0 if fresh else 1) :]
    out_ref, scratch = refs[0], refs[1:]
    first_site = lax.axis_index("site") == 0
    if fresh:
        out_ref[...] = jnp.zeros(out_ref.shape, out_ref.dtype)
    for ref, (d, first, kind) in zip(held, pieces):
        place = functools.partial(place_blocks, table_ref, d, first, out_ref=out_ref)
        if kind == "always":
            place(ref)
        elif kind == "rest":

            @pl.when(table_ref[d, table_ref.shape[1] - 1] > first)
            def _(ref=ref, place=place):
                spare_ref, sem = scratch
                copy = pltpu.make_async_copy(ref, spare_ref, sem)
                copy.start()
                copy.wait()
                place(spare_ref)

        else:

            @pl.when(first_site if kind == "first" else ~first_site)
            def _(ref=ref, place=place):
                place(ref)


def unpack(table, pieces, extras, weights, bond):
    fresh = weights is None
    operands = [piece[0] for piece in pieces] + list(extras)
    in_specs = [HBM if piece[3] == "rest" else VMEM for piece in pieces] + [HBM] * len(extras)
    aliases = {}
    if not fresh:
        operands.append(weights)
        in_specs.append(VMEM)
        aliases = {len(operands): 0}
    rest = [piece[0] for piece in pieces if piece[3] == "rest"]
    scratch = [pltpu.VMEM(rest[0].shape, rest[0].dtype), pltpu.SemaphoreType.DMA] if rest else []
    dtype = pieces[0][0].dtype
    return pl.pallas_call(
        functools.partial(unpack_kernel, [piece[1:] for piece in pieces], len(extras), fresh),
        out_shape=pltpu.VMEM((bond, bond), dtype),
        grid_spec=pltpu.PrefetchScalarGridSpec(
            num_scalar_prefetch=1,
            grid=(1,),
            in_specs=in_specs,
            out_specs=VMEM,
            scratch_shapes=scratch,
        ),
        input_output_aliases=aliases,
        compiler_params=pltpu.CompilerParams(vmem_limit_bytes=24 * 1024 * 1024),
        cost_estimate=pl.CostEstimate(
            flops=0,
            bytes_accessed=4 * sum(piece[0].size for piece in pieces if piece[3] != "rest"),
            transcendentals=0,
        ),
    )(table, *operands)


def blank(shape, dtype, count):
    return pl.pallas_call(
        lambda *refs: None,
        out_shape=(jax.ShapeDtypeStruct(shape, dtype),) * count,
        out_specs=(HBM,) * count,
        compiler_params=pltpu.CompilerParams(vmem_limit_bytes=1024 * 1024),
    )()


def step_kernel(chunks, step, relay, carried, ends, right_ref, *refs):
    refs = list(refs)
    first_ref, picks_ref, left_ref = refs[:3]
    weights = refs[3 : 3 + chunks]
    refs = refs[3 + chunks :]
    received_ref = refs.pop(0) if relay else None
    if carried:
        old_ref, old_norm_ref = refs[:2]
        refs = refs[4:]
    sent_ref, norm_ref, fronts_ref, norms_ref, lhs_ref, acc_ref, sems = refs
    rows, bond = sent_ref.shape
    site = lax.axis_index("site")
    micro = step - DELAY * site
    micro_count = first_ref.shape[0] // rows

    def active(back):
        return (micro >= back) & (micro < micro_count + back)

    tile = min(bond, 512)

    def copies(back, front_ref, row_norm_ref):
        where = pl.ds(pl.multiple_of((micro - back) * rows, 8), rows)
        return (
            pltpu.make_async_copy(front_ref, fronts_ref.at[where], sems.at[0]),
            pltpu.make_async_copy(row_norm_ref, norms_ref.at[where], sems.at[1]),
        )

    if carried:

        @pl.when(active(1))
        def _():
            for copy in copies(1, old_ref, old_norm_ref):
                copy.start()

    @pl.when(active(0))
    def _():
        here = pl.ds(pl.multiple_of(micro * rows, 8), rows)
        front = first_ref[here, :].astype(jnp.float32)
        if relay:
            front = jnp.where(site == 0, front, received_ref[...].astype(jnp.float32))
        charge = (left_ref[...] + picks_ref[here, :]) & (CHARGES - 1)
        for q in range(CHARGES):
            lhs_ref[q * rows : (q + 1) * rows, :] = jnp.where(charge == q, front, 0.0).astype(
                jnp.bfloat16
            )
        for n in range(bond // tile):
            cols = slice(n * tile, (n + 1) * tile)
            total = jnp.zeros((CHARGES * rows, tile), jnp.float32)
            low = 0
            for part in weights:
                high = low + part.shape[0]
                total += jnp.dot(
                    lhs_ref[:, low:high], part[:, cols], preferred_element_type=jnp.float32
                )
                low = high
            acc_ref[:, cols] = total

        def chosen(j):
            first = pl.multiple_of(right_ref[j] * rows, 8)
            return acc_ref[pl.ds(first, rows), j * BLOCK : (j + 1) * BLOCK]

        squares = jnp.zeros((rows, LANES), jnp.float32)
        for j in range(bond // BLOCK):
            squares += chosen(j) * chosen(j)
        norm = jnp.sqrt(jnp.sum(squares, axis=1, keepdims=True) / bond + EPSILON)
        norm_ref[...] = jnp.broadcast_to(norm, norm_ref.shape)
        for j in range(bond // BLOCK):
            sent_ref[:, j * BLOCK : (j + 1) * BLOCK] = (chosen(j) / norm).astype(sent_ref.dtype)

    if carried:

        @pl.when(active(1))
        def _():
            for copy in copies(1, old_ref, old_norm_ref):
                copy.wait()

    if ends:

        @pl.when(active(0))
        def _():
            for copy in copies(0, sent_ref, norm_ref):
                copy.start()
            for copy in copies(0, sent_ref, norm_ref):
                copy.wait()


def advance(step, ends, right, fronts_in, picks, left, weights, received, old, results):
    row_count, bond = fronts_in.shape
    rows = MICRO
    relay = received is not None
    carried = results is not None
    operands = [fronts_in, picks, left, *weights]
    in_specs = [VMEM] * len(operands)
    aliases = {}
    if relay:
        operands.append(received)
        in_specs.append(VMEM)
    if carried:
        operands += [*old, *results]
        in_specs += [VMEM, VMEM, HBM, HBM]
        aliases = {len(operands) - 1: 2, len(operands): 3}
    return pl.pallas_call(
        functools.partial(step_kernel, len(weights), step, relay, carried, ends),
        out_shape=(
            jax.ShapeDtypeStruct((rows, bond), jnp.bfloat16),
            jax.ShapeDtypeStruct((rows, LANES), jnp.float32),
            jax.ShapeDtypeStruct((row_count, bond), jnp.bfloat16),
            jax.ShapeDtypeStruct((row_count, LANES), jnp.float32),
        ),
        grid_spec=pltpu.PrefetchScalarGridSpec(
            num_scalar_prefetch=1,
            grid=(1,),
            in_specs=in_specs,
            out_specs=(VMEM, VMEM, HBM, HBM),
            scratch_shapes=[
                pltpu.VMEM((CHARGES * rows, bond), jnp.bfloat16),
                pltpu.VMEM((CHARGES * rows, bond), jnp.float32),
                pltpu.SemaphoreType.DMA((2,)),
            ],
        ),
        input_output_aliases=aliases,
        compiler_params=pltpu.CompilerParams(vmem_limit_bytes=24 * 1024 * 1024),
        cost_estimate=pl.CostEstimate(
            flops=2 * CHARGES * rows * bond * bond,
            bytes_accessed=2 * bond * bond,
            transcendentals=0,
        ),
    )(right, *operands)


def gather_weights(site_tensor, charges, extras):
    shards = lax.axis_size("sample")
    sites = lax.axis_size("site")
    groups = lax.axis_size("groups")
    cores = 2 if shards % 2 == 0 else 1
    chips = shards // cores
    bond = site_tensor.shape[1]
    blocks = bond // BLOCK
    per_shard = site_tensor.shape[3] // BLOCK
    total = blocks * per_shard
    unit = total // 16
    early, turn, cap = 6 * unit, 6 * unit + 3 * unit, 12 * unit
    if sites == 1:
        turn = early
    spans = [(0, early), (early, turn), (turn, cap), (early, cap)]

    def to(hop, i):
        return ((i // cores - hop) % chips) * cores + i % cores

    def move(part, pairs):
        flat = [(s * shards + i, t * shards + j) for (s, i), (t, j) in pairs]
        return lax.ppermute(part, ("site", "sample"), flat)

    everyone = [(s, i) for s in range(sites) for i in range(shards)]

    def across_chips(part, up, among):
        return [
            move(part, [((s, i), (s + up, to(hop, i))) for s, i in everyone if s in among])
            for hop in range(1, chips)
        ]

    def across_cores(part):
        return lax.ppermute(part, "sample", [(i, i ^ 1) for i in range(shards)])

    def with_cores(parts, first, kind):
        pieces = []
        for hop, part in enumerate(parts, 1):
            pieces.append((part, hop * cores, first, kind))
            if cores == 2:
                pieces.append((across_cores(part), hop * cores + 1, first, kind))
        return pieces

    packed, head, detour, tail, late = pick(site_tensor, charges, spans)
    one, others, relay = range(1), range(1, sites), min(3, sites - 1)
    head = across_chips(head, 0, range(sites))
    tail = across_chips(tail, 0, one)
    away = across_chips(detour, relay, one)
    late = across_chips(late, 0, others)

    table = plan(charges, blocks, per_shard, cores, shards)
    outcome = (charges[1:, None, :] - charges[:-1, :, None]) & (CHARGES - 1)
    held = jnp.sum((outcome < 2).reshape(sites, blocks, shards, per_shard), axis=(1, 3))
    mine = jnp.max(held.astype(jnp.int32)).reshape(1)
    most = mine
    for hop in range(1, groups):
        pairs = [(i, (i + hop) % groups) for i in range(groups)]
        most = jnp.maximum(most, lax.ppermute(mine, "groups", pairs))

    rest_shape = ((total - cap) * BLOCK, BLOCK)

    def send_rest(blocks):
        parts = across_chips(blocks[cap * BLOCK : total * BLOCK], 0, range(sites))
        return tuple(piece[0] for piece in with_cores(parts, cap, "rest"))

    def keep(blocks):
        return tuple(blank(rest_shape, blocks.dtype, (chips - 1) * cores))

    rest = lax.cond(most[0] > cap, send_rest, keep, packed) if chips > 1 else ()
    rest = [(part, cores + k, cap, "rest") for k, part in enumerate(rest)]

    local = [(packed, 0, 0, "always")]
    if cores == 2:
        local.append((across_cores(packed), 1, 0, "always"))
    weights = unpack(table, local, [*extras, *[piece[0] for piece in rest]], None, bond)

    home = [move(part, [((relay, i), (0, i)) for i in range(shards)]) for part in away]
    head, weights = lax.optimization_barrier((head, weights))
    pieces = with_cores(head, 0, "always")
    weights = unpack(table, pieces, [], weights, bond)
    (tail, home), weights = lax.optimization_barrier(((tail, home), weights))
    pieces = with_cores(home, early, "first")
    pieces += with_cores(tail, turn, "first")
    weights = unpack(table, pieces + rest, [], weights, bond)

    def exchange(after):
        parts, after = lax.optimization_barrier((late, after))
        return with_cores(parts, early, "others")

    def complete(weights, pieces, after):
        return unpack(table, pieces, [after], weights, bond)

    return weights, exchange, complete


def pipeline(site_tensor, fronts_in, outcomes, charges):
    owner = lax.axis_index("site")
    sites = lax.axis_size("site")
    left = lax.dynamic_index_in_dim(charges, owner, 0, keepdims=False)
    right = lax.dynamic_index_in_dim(charges, owner + 1, 0, keepdims=False)
    row_count, _ = fronts_in.shape
    micro_count = row_count // MICRO
    picks = outcomes[0][:, None]
    left_lanes = jnp.repeat(left, BLOCK)[None, :]
    steps = micro_count + DELAY * (sites - 1)
    weights, exchange, complete = gather_weights(site_tensor, charges, [picks, left_lanes, right])
    received, old, results = {}, None, None
    for step in range(steps):
        if step == DELAY - 1:
            late = exchange(old[0])
        if step == DELAY:
            weights = complete(weights, late, old[0])
        sent, norm, *results = advance(
            step, step == steps - 1, right, fronts_in, picks, left_lanes, [weights],
            received.pop(step - DELAY, None), old, results,
        )
        old = (sent, norm)
        pairs = [
            (s, s + 1) for s in range(sites - 1) if 0 <= step - DELAY * s < micro_count
        ]
        if pairs:
            received[step] = lax.ppermute(sent, "site", pairs)
    fronts, norms = results
    return fronts[None], jnp.log(norms[:, 0])[None]


def solution(mesh):
    in_specs = (
        P(("groups", "site"), None, None, "sample"),
        P(("groups", "sample"), None),
        P(("groups", "site"), "sample"),
        P("groups", None),
    )
    out_specs = (P(("groups", "site"), "sample", None), P(("groups", "site"), "sample"))
    return jax.shard_map(
        pipeline, mesh=mesh, in_specs=in_specs, out_specs=out_specs, check_vma=False
    )
```

```python
import functools

import jax
import jax.numpy as jnp
from jax import lax
from jax.experimental import pallas as pl
from jax.experimental.pallas import tpu as pltpu
from jax.sharding import PartitionSpec as P

BLOCK = 128
CHARGES = 4
LANES = 128
SHIFT = 12
EPSILON = 1e-06
MICRO = 48
DELAY = 3


VMEM = pl.BlockSpec(memory_space=pltpu.VMEM)
HBM = pl.BlockSpec(memory_space=pl.ANY)


def allowed_outcome(charge_ref, site, i, j):
    return (charge_ref[site + 1, j] - charge_ref[site, i]) & (CHARGES - 1)


def pick_kernel(blocks, starts, charge_ref, tensor_ref, packed_ref, *refs):
    *out_refs, both_ref = refs
    width = tensor_ref.shape[3]
    per_shard = width // BLOCK
    site = lax.axis_index("site")
    mine = lax.axis_index("sample") * per_shard
    row = lax.broadcasted_iota(jnp.int32, (2 * BLOCK, 2 * BLOCK), 0)
    col = lax.broadcasted_iota(jnp.int32, (2 * BLOCK, 2 * BLOCK), 1)
    source = jnp.where(row < BLOCK, 2 * row, 2 * (row - BLOCK) + 1)
    select = jnp.where(col == source, 1.0, 0.0).astype(jnp.bfloat16)
    both_ref[...] = select
    entry = jnp.int32(0)
    for i in range(blocks):
        pairs = tensor_ref[0, i * BLOCK : (i + 1) * BLOCK, :, :].reshape(2 * BLOCK, width)
        for j in range(per_shard):
            outcome = allowed_outcome(charge_ref, site, i, mine + j)
            start = pl.multiple_of(jnp.minimum(outcome, 1) * BLOCK, BLOCK)
            there = pl.ds(pl.multiple_of(entry * BLOCK, BLOCK), BLOCK)
            packed_ref[there, :] = jnp.dot(
                both_ref[pl.ds(start, BLOCK), :],
                pairs[:, j * BLOCK : (j + 1) * BLOCK],
                preferred_element_type=jnp.float32,
            ).astype(jnp.bfloat16)
            entry += (outcome < 2).astype(jnp.int32)
    for start, out_ref in zip(starts, out_refs):
        low = start * BLOCK
        out_ref[...] = packed_ref[low : low + out_ref.shape[0], :]


def pick(tensor, charges, spans):
    _, bond, _, width = tensor.shape
    blocks = bond // BLOCK
    total = blocks * (width // BLOCK)
    return pl.pallas_call(
        functools.partial(pick_kernel, blocks, [low for low, _ in spans]),
        out_shape=tuple(
            pltpu.VMEM((count * BLOCK, BLOCK), tensor.dtype)
            for count in (total + 1, *[high - low for low, high in spans])
        ),
        grid_spec=pltpu.PrefetchScalarGridSpec(
            num_scalar_prefetch=1,
            grid=(1,),
            in_specs=[VMEM],
            out_specs=(VMEM,) * (1 + len(spans)),
            scratch_shapes=[pltpu.VMEM((2 * BLOCK, 2 * BLOCK), jnp.bfloat16)],
        ),
        compiler_params=pltpu.CompilerParams(vmem_limit_bytes=16 * 1024 * 1024),
        cost_estimate=pl.CostEstimate(
            flops=8 * bond * width * BLOCK, bytes_accessed=6 * bond * width, transcendentals=0
        ),
    )(charges, tensor)


def plan_kernel(blocks, per_shard, cores, charge_ref, table_ref):
    shards, _ = table_ref.shape
    chips = shards // cores
    me = lax.axis_index("sample")
    site = lax.axis_index("site")
    total = blocks * per_shard
    for d in range(shards):
        chip = lax.rem(me // cores + d // cores, chips)
        first = (chip * cores + lax.rem(me + d, cores)) * per_shard

        def one(i, entry):
            for j in range(per_shard):
                table_ref[d, entry] = (i << SHIFT) + first + j
                allowed = allowed_outcome(charge_ref, site, i, first + j) < 2
                entry += allowed.astype(jnp.int32)
            return entry

        count = lax.fori_loop(0, blocks, one, jnp.int32(0))
        table_ref[d, total + 1] = count


def plan(charges, blocks, per_shard, cores, shards):
    size = blocks * per_shard + 2
    return pl.pallas_call(
        functools.partial(plan_kernel, blocks, per_shard, cores),
        out_shape=jax.ShapeDtypeStruct((shards, size), jnp.int32),
        grid_spec=pltpu.PrefetchScalarGridSpec(
            num_scalar_prefetch=1,
            grid=(1,),
            in_specs=[],
            out_specs=pl.BlockSpec(memory_space=pltpu.SMEM),
        ),
        compiler_params=pltpu.CompilerParams(vmem_limit_bytes=1024 * 1024),
        cost_estimate=pl.CostEstimate(flops=100, bytes_accessed=4096, transcendentals=0),
    )(charges)


def place_blocks(table_ref, d, first, ref, out_ref):
    total = table_ref.shape[1] - 2
    size = min(ref.shape[0] // BLOCK, total - first)

    def one(e, carry):
        spot = table_ref[d, first + e]
        rows = pl.ds(pl.multiple_of((spot >> SHIFT) * BLOCK, BLOCK), BLOCK)
        cols = pl.ds(pl.multiple_of((spot & ((1 << SHIFT) - 1)) * BLOCK, BLOCK), BLOCK)
        out_ref[rows, cols] = ref[pl.ds(pl.multiple_of(e * BLOCK, BLOCK), BLOCK), :]
        return carry

    lax.fori_loop(0, jnp.clip(table_ref[d, total + 1] - first, 0, size), one, 0)


def unpack_kernel(pieces, extras, fresh, table_ref, *refs):
    refs = list(refs)
    held, refs = refs[: len(pieces)], refs[len(pieces) + extras + (0 if fresh else 1) :]
    out_ref, scratch = refs[0], refs[1:]
    first_site = lax.axis_index("site") == 0
    if fresh:
        out_ref[...] = jnp.zeros(out_ref.shape, out_ref.dtype)
    for ref, (d, first, kind) in zip(held, pieces):
        place = functools.partial(place_blocks, table_ref, d, first, out_ref=out_ref)
        if kind == "always":
            place(ref)
        elif kind == "rest":

            @pl.when(table_ref[d, table_ref.shape[1] - 1] > first)
            def _(ref=ref, place=place):
                spare_ref, sem = scratch
                copy = pltpu.make_async_copy(ref, spare_ref, sem)
                copy.start()
                copy.wait()
                place(spare_ref)

        else:

            @pl.when(first_site if kind == "first" else ~first_site)
            def _(ref=ref, place=place):
                place(ref)


def unpack(table, pieces, extras, weights, bond):
    fresh = weights is None
    operands = [piece[0] for piece in pieces] + list(extras)
    in_specs = [HBM if piece[3] == "rest" else VMEM for piece in pieces] + [HBM] * len(extras)
    aliases = {}
    if not fresh:
        operands.append(weights)
        in_specs.append(VMEM)
        aliases = {len(operands): 0}
    rest = [piece[0] for piece in pieces if piece[3] == "rest"]
    scratch = [pltpu.VMEM(rest[0].shape, rest[0].dtype), pltpu.SemaphoreType.DMA] if rest else []
    dtype = pieces[0][0].dtype
    return pl.pallas_call(
        functools.partial(unpack_kernel, [piece[1:] for piece in pieces], len(extras), fresh),
        out_shape=pltpu.VMEM((bond, bond), dtype),
        grid_spec=pltpu.PrefetchScalarGridSpec(
            num_scalar_prefetch=1,
            grid=(1,),
            in_specs=in_specs,
            out_specs=VMEM,
            scratch_shapes=scratch,
        ),
        input_output_aliases=aliases,
        compiler_params=pltpu.CompilerParams(vmem_limit_bytes=24 * 1024 * 1024),
        cost_estimate=pl.CostEstimate(
            flops=0,
            bytes_accessed=4 * sum(piece[0].size for piece in pieces if piece[3] != "rest"),
            transcendentals=0,
        ),
    )(table, *operands)


def blank(shape, dtype, count):
    return pl.pallas_call(
        lambda *refs: None,
        out_shape=(jax.ShapeDtypeStruct(shape, dtype),) * count,
        out_specs=(HBM,) * count,
        compiler_params=pltpu.CompilerParams(vmem_limit_bytes=1024 * 1024),
    )()


def step_kernel(chunks, step, relay, carried, ends, right_ref, *refs):
    refs = list(refs)
    first_ref, picks_ref, left_ref = refs[:3]
    weights = refs[3 : 3 + chunks]
    refs = refs[3 + chunks :]
    received_ref = refs.pop(0) if relay else None
    if carried:
        old_ref, old_norm_ref = refs[:2]
        refs = refs[4:]
    if ends:
        fronts_ref, norms_ref, sent_ref, norm_ref, lhs_ref, acc_ref, sems = refs
    else:
        sent_ref, norm_ref, fronts_ref, norms_ref, lhs_ref, acc_ref, sems = refs
    rows, bond = sent_ref.shape
    site = lax.axis_index("site")
    micro = step - DELAY * site
    micro_count = first_ref.shape[0] // rows

    def active(back):
        return (micro >= back) & (micro < micro_count + back)

    tile = min(bond, 512)

    def piece(n):
        where = pl.ds(pl.multiple_of(micro * rows, 8), rows)
        cols = slice(n * tile, (n + 1) * tile)
        return pltpu.make_async_copy(
            sent_ref.at[:, cols], fronts_ref.at[where, cols], sems.at[4 + n]
        )

    def copies(back, front_ref, row_norm_ref):
        where = pl.ds(pl.multiple_of((micro - back) * rows, 8), rows)
        return (
            pltpu.make_async_copy(front_ref, fronts_ref.at[where], sems.at[2 * back]),
            pltpu.make_async_copy(row_norm_ref, norms_ref.at[where], sems.at[2 * back + 1]),
        )

    if carried:

        @pl.when(active(1))
        def _():
            for copy in copies(1, old_ref, old_norm_ref):
                copy.start()

    @pl.when(active(0))
    def _():
        here = pl.ds(pl.multiple_of(micro * rows, 8), rows)
        front = first_ref[here, :].astype(jnp.float32)
        if relay:
            front = jnp.where(site == 0, front, received_ref[...].astype(jnp.float32))
        charge = (left_ref[...] + picks_ref[here, :]) & (CHARGES - 1)
        for q in range(CHARGES):
            lhs_ref[q * rows : (q + 1) * rows, :] = jnp.where(charge == q, front, 0.0).astype(
                jnp.bfloat16
            )
        for n in range(bond // tile):
            cols = slice(n * tile, (n + 1) * tile)
            total = jnp.zeros((CHARGES * rows, tile), jnp.float32)
            low = 0
            for part in weights:
                high = low + part.shape[0]
                total += jnp.dot(
                    lhs_ref[:, low:high], part[:, cols], preferred_element_type=jnp.float32
                )
                low = high
            acc_ref[:, cols] = total

        def chosen(j):
            first = pl.multiple_of(right_ref[j] * rows, 8)
            return acc_ref[pl.ds(first, rows), j * BLOCK : (j + 1) * BLOCK]

        squares = jnp.zeros((rows, LANES), jnp.float32)
        for j in range(bond // BLOCK):
            squares += chosen(j) * chosen(j)
        norm = jnp.sqrt(jnp.sum(squares, axis=1, keepdims=True) / bond + EPSILON)
        norm_ref[...] = jnp.broadcast_to(norm, norm_ref.shape)
        if ends:
            copies(0, sent_ref, norm_ref)[1].start()
        for j in range(bond // BLOCK):
            sent_ref[:, j * BLOCK : (j + 1) * BLOCK] = (chosen(j) / norm).astype(sent_ref.dtype)
            if ends and (j + 1) % (tile // BLOCK) == 0:
                piece((j + 1) * BLOCK // tile - 1).start()

    if carried:

        @pl.when(active(1))
        def _():
            for copy in copies(1, old_ref, old_norm_ref):
                copy.wait()

    if ends:

        @pl.when(active(0))
        def _():
            copies(0, sent_ref, norm_ref)[1].wait()
            for n in range(bond // tile):
                piece(n).wait()


def advance(step, ends, right, fronts_in, picks, left, weights, received, old, results):
    row_count, bond = fronts_in.shape
    rows = MICRO
    relay = received is not None
    carried = results is not None
    rounds = (pltpu.VMEM((rows, bond), jnp.bfloat16), pltpu.VMEM((rows, LANES), jnp.float32))
    operands = [fronts_in, picks, left, *weights]
    in_specs = [VMEM] * len(operands)
    aliases = {}
    if relay:
        operands.append(received)
        in_specs.append(VMEM)
    if carried:
        operands += [*old, *results]
        in_specs += [VMEM, VMEM, HBM, HBM]
        aliases = {len(operands) - 1: 0 if ends else 2, len(operands): 1 if ends else 3}
    return pl.pallas_call(
        functools.partial(step_kernel, len(weights), step, relay, carried, ends),
        out_shape=(
            *(() if ends else (jax.ShapeDtypeStruct(r.shape, r.dtype) for r in rounds)),
            jax.ShapeDtypeStruct((row_count, bond), jnp.bfloat16),
            jax.ShapeDtypeStruct((row_count, LANES), jnp.float32),
        ),
        grid_spec=pltpu.PrefetchScalarGridSpec(
            num_scalar_prefetch=1,
            grid=(1,),
            in_specs=in_specs,
            out_specs=(HBM, HBM) if ends else (VMEM, VMEM, HBM, HBM),
            scratch_shapes=[
                *(rounds if ends else ()),
                pltpu.VMEM((CHARGES * rows, bond), jnp.bfloat16),
                pltpu.VMEM((CHARGES * rows, bond), jnp.float32),
                pltpu.SemaphoreType.DMA((4 + bond // min(bond, 512),)),
            ],
        ),
        input_output_aliases=aliases,
        compiler_params=pltpu.CompilerParams(vmem_limit_bytes=24 * 1024 * 1024),
        cost_estimate=pl.CostEstimate(
            flops=2 * CHARGES * rows * bond * bond,
            bytes_accessed=2 * bond * bond,
            transcendentals=0,
        ),
    )(right, *operands)


def gather_weights(site_tensor, charges, extras):
    shards = lax.axis_size("sample")
    sites = lax.axis_size("site")
    groups = lax.axis_size("groups")
    cores = 2 if shards % 2 == 0 else 1
    chips = shards // cores
    bond = site_tensor.shape[1]
    blocks = bond // BLOCK
    per_shard = site_tensor.shape[3] // BLOCK
    total = blocks * per_shard
    unit = total // 16
    early, turn, cap = 6 * unit, 6 * unit + 3 * unit, 12 * unit
    if sites == 1:
        turn = early
    spans = [(0, early), (early, turn), (turn, cap), (early, cap)]

    def to(hop, i):
        return ((i // cores - hop) % chips) * cores + i % cores

    def move(part, pairs):
        flat = [(s * shards + i, t * shards + j) for (s, i), (t, j) in pairs]
        return lax.ppermute(part, ("site", "sample"), flat)

    everyone = [(s, i) for s in range(sites) for i in range(shards)]

    def across_chips(part, up, among):
        return [
            move(part, [((s, i), (s + up, to(hop, i))) for s, i in everyone if s in among])
            for hop in range(1, chips)
        ]

    def across_cores(part):
        return lax.ppermute(part, "sample", [(i, i ^ 1) for i in range(shards)])

    def with_cores(parts, first, kind):
        pieces = []
        for hop, part in enumerate(parts, 1):
            pieces.append((part, hop * cores, first, kind))
            if cores == 2:
                pieces.append((across_cores(part), hop * cores + 1, first, kind))
        return pieces

    packed, head, detour, tail, late = pick(site_tensor, charges, spans)
    one, others, relay = range(1), range(1, sites), min(3, sites - 1)
    head = across_chips(head, 0, range(sites))
    tail = across_chips(tail, 0, one)
    away = across_chips(detour, relay, one)
    late = across_chips(late, 0, others)

    table = plan(charges, blocks, per_shard, cores, shards)
    outcome = (charges[1:, None, :] - charges[:-1, :, None]) & (CHARGES - 1)
    held = jnp.sum((outcome < 2).reshape(sites, blocks, shards, per_shard), axis=(1, 3))
    mine = jnp.max(held.astype(jnp.int32)).reshape(1)
    most = mine
    for hop in range(1, groups):
        pairs = [(i, (i + hop) % groups) for i in range(groups)]
        most = jnp.maximum(most, lax.ppermute(mine, "groups", pairs))

    rest_shape = ((total - cap) * BLOCK, BLOCK)

    def send_rest(blocks):
        parts = across_chips(blocks[cap * BLOCK : total * BLOCK], 0, range(sites))
        return tuple(piece[0] for piece in with_cores(parts, cap, "rest"))

    def keep(blocks):
        return tuple(blank(rest_shape, blocks.dtype, (chips - 1) * cores))

    rest = lax.cond(most[0] > cap, send_rest, keep, packed) if chips > 1 else ()
    rest = [(part, cores + k, cap, "rest") for k, part in enumerate(rest)]

    local = [(packed, 0, 0, "always")]
    if cores == 2:
        local.append((across_cores(packed), 1, 0, "always"))
    weights = unpack(table, local, [*extras, *[piece[0] for piece in rest]], None, bond)

    home = [move(part, [((relay, i), (0, i)) for i in range(shards)]) for part in away]
    head, weights = lax.optimization_barrier((head, weights))
    pieces = with_cores(head, 0, "always")
    weights = unpack(table, pieces, [], weights, bond)
    (tail, home), weights = lax.optimization_barrier(((tail, home), weights))
    pieces = with_cores(home, early, "first")
    pieces += with_cores(tail, turn, "first")
    weights = unpack(table, pieces + rest, [], weights, bond)

    def exchange(after):
        parts, after = lax.optimization_barrier((late, after))
        return with_cores(parts, early, "others")

    def complete(weights, pieces, after):
        return unpack(table, pieces, [after], weights, bond)

    return weights, exchange, complete


def pipeline(site_tensor, fronts_in, outcomes, charges):
    owner = lax.axis_index("site")
    sites = lax.axis_size("site")
    left = lax.dynamic_index_in_dim(charges, owner, 0, keepdims=False)
    right = lax.dynamic_index_in_dim(charges, owner + 1, 0, keepdims=False)
    row_count, _ = fronts_in.shape
    micro_count = row_count // MICRO
    picks = outcomes[0][:, None]
    left_lanes = jnp.repeat(left, BLOCK)[None, :]
    steps = micro_count + DELAY * (sites - 1)
    weights, exchange, complete = gather_weights(site_tensor, charges, [picks, left_lanes, right])
    received, old, results = {}, None, None
    for step in range(steps):
        if step == DELAY - 1:
            late = exchange(old[0])
        if step == DELAY:
            weights = complete(weights, late, old[0])
        *old, fronts, norms = advance(
            step, step == steps - 1, right, fronts_in, picks, left_lanes, [weights],
            received.pop(step - DELAY, None), old, results,
        )
        results = (fronts, norms)
        pairs = [
            (s, s + 1) for s in range(sites - 1) if 0 <= step - DELAY * s < micro_count
        ]
        if pairs:
            received[step] = lax.ppermute(old[0], "site", pairs)
    return fronts[None], jnp.log(norms[:, 0])[None]


def solution(mesh):
    in_specs = (
        P(("groups", "site"), None, None, "sample"),
        P(("groups", "sample"), None),
        P(("groups", "site"), "sample"),
        P("groups", None),
    )
    out_specs = (P(("groups", "site"), "sample", None), P(("groups", "site"), "sample"))
    return jax.shard_map(
        pipeline, mesh=mesh, in_specs=in_specs, out_specs=out_specs, check_vma=False
    )
```
